32 devices in a mesh: row: 8 (over y, x, core), col: 4 (over z).
Axes of the slice: x: 2, y: 2, z: 4, core: 2. Of those that a mesh axis runs over, the one named last changes fastest.
Arguments:
- features: float32 [4096, 128], P(('row', 'col')), may hold values from -6 to 6
- weight: float32 [128, 128], replicated, may hold values from -0.5 to 0.5
- layer_bias: float32 [128], replicated, may hold values from -3 to 3
- degree_scale: float32 [4096], P(('row', 'col')), may hold values from 0.05 to 0.5
- tile_values: bfloat16 [8, 4, 32, 128, 128], P('row', 'col'), may hold values from 0 to 1
- tile_slots: int32 [8, 4, 32], P('row', 'col'), may hold values from 0 to 31, as said below
- tile_count: int32 [8, 4], P('row', 'col'), may hold values from 1 to 32, as said below
- cotangent: float32 [4096, 128], P(('row', 'col')), may hold values from -6 to 6
Outputs:
- activations: float32 [4096, 128], P(('row', 'col'))
- feature_grad: float32 [4096, 128], P(('row', 'col'))
- weight_grad: float32 [128, 128], replicated
- bias_grad: float32 [128], replicated
The draws below stay inside these ranges and needn't reach their ends.
Inputs may be any that keep to these rules, and one draw needn't show every extreme that they name: `tile_slots`: the first tile_count[r, c] slots of a device name distinct positions of its grid of 8 by 4 tiles (row u, column v as p = u * 4 + v); later slots hold other positions in range and are ignored. `tile_count`: counts are skewed across devices; in every draw some device has a full list of 32 tiles.
All inputs are finite; a program needn't handle non-finite values.
Results may differ from the reference program's by a relative error of at most 0.0059.
Values may be sent and summed in bfloat16 or wider, within the bound.
A program may use at most 64 MiB of HBM per device.

```python
import math
import jax
import jax.numpy as jnp
from jax import lax

F = 128
TILE = 128
NBD = 1
MAXT = 32
NODES = 4096
N_ROW = 8
N_COL = 4


def tile_layout(key):
    devices = N_ROW * N_COL
    positions = N_ROW * NBD * N_COL * NBD
    subkeys = jax.random.split(jax.random.fold_in(key, 7), devices)

    def one_device(subkey):
        return jax.random.permutation(subkey, positions)[:MAXT]
    placed = jax.vmap(one_device)(subkeys)
    drawn = jax.random.randint(jax.random.fold_in(key, 11), (devices,), 0, MAXT)
    tile_counts = 1 + drawn * drawn // MAXT
    busiest = jax.random.randint(jax.random.fold_in(key, 13), (), 0, devices)
    tile_counts = jnp.where(jnp.arange(devices) == busiest, MAXT, tile_counts)
    return (placed.reshape(N_ROW, N_COL, MAXT).astype(jnp.int32), tile_counts.reshape(N_ROW, N_COL).astype(jnp.int32))


def draw_tile_slots(key, part):
    placed, tile_counts = tile_layout(key)
    return placed


def draw_tile_count(key, part):
    placed, tile_counts = tile_layout(key)
    return tile_counts


def block_levels(stream_key, shape, cuts, low, largest):
    def one(axis_at, blocks):
        steps = jax.random.uniform(jax.random.fold_in(jax.random.fold_in(stream_key, 6), axis_at), (blocks,), jnp.float32, low / len(cuts), largest / len(cuts))
        return jnp.repeat(jnp.exp(steps), shape[axis_at] // blocks).reshape((-1,) + (1,) * (len(shape) - axis_at - 1))

    level = one(*cuts[0])
    for cut in cuts[1:]:
        level = level * one(*cut)
    return level


def centred(key, shape, deviation, reach, cuts=(), kind=jnp.bfloat16):
    loudness = block_levels(key, shape, cuts, -0.22, 0.18) if cuts else 1.0
    values = jax.random.normal(key, shape, jnp.float32) * deviation * loudness
    return jnp.minimum(jnp.maximum(values, -reach), reach).astype(kind)


def setup_inputs(seed: int = 0) -> dict:
    key_of = jax.random.split(jax.random.key(seed), 9)
    features = centred(key_of[0], (NODES, F), 1.0, 6.0, ((0, 32),), jnp.float32)
    weight = centred(key_of[1], (F, F), F ** -0.5, 0.5, (), jnp.float32)
    layer_bias = centred(key_of[2], (F,), 0.5, 3.0, (), jnp.float32)
    degree_scale = jnp.clip(jnp.exp(math.log(0.5) - 2.3025851 * jax.random.uniform(key_of[3], (NODES,), jnp.float32) ** block_levels(key_of[3], (NODES,), ((0, 32),), -0.2, 0.2)), 0.05, 0.5)
    tile_values = jnp.clip(1.0 * jax.random.uniform(key_of[4], (N_ROW, N_COL, MAXT, TILE, TILE), jnp.float32) ** block_levels(key_of[4], (N_ROW, N_COL, MAXT, TILE, TILE), ((0, 8), (1, 4)), -0.2, 0.2), 0.0, 1.0).astype(jnp.bfloat16)
    tile_slots = draw_tile_slots(jax.random.fold_in(key_of[8], 71), 0)
    tile_count = draw_tile_count(jax.random.fold_in(key_of[8], 71), 0)
    cotangent = centred(key_of[7], (NODES, F), 1.0, 6.0, ((0, 32),), jnp.float32)
    return dict(features=features, weight=weight, layer_bias=layer_bias, degree_scale=degree_scale, tile_values=tile_values, tile_slots=tile_slots, tile_count=tile_count, cotangent=cotangent)


def gelu_pair(values):
    argument = 0.7978845608028654 * (values + 0.044715 * values * values * values)
    tangent = jnp.tanh(argument)
    output = 0.5 * values * (1.0 + tangent)
    slopes = 0.5 * (1.0 + tangent) + 0.5 * values * (1.0 - tangent * tangent) * 0.7978845608028654 * (1.0 + 3.0 * 0.044715 * values * values)
    return (output, slopes)

def reference(features, weight, layer_bias, degree_scale, tile_values, tile_slots, tile_count, cotangent):
    highest = lax.Precision.HIGHEST
    devices = N_ROW * N_COL
    column_blocks = N_COL * NBD
    node_blocks = devices * NBD
    nodes = node_blocks * TILE
    norm_factor = 1.0 / math.sqrt(nodes)
    slots_flat = tile_slots.reshape(devices, MAXT)
    counts_flat = tile_count.reshape(devices)
    values_flat = tile_values.reshape(devices, MAXT, TILE, TILE)

    def placement(device):
        row_index = device // N_COL
        col_index = device % N_COL
        slots = slots_flat[device]
        local_rows = slots // column_blocks
        local_cols = slots % column_blocks
        global_rows = (local_rows // NBD * N_COL + col_index) * NBD + local_rows % NBD
        global_cols = row_index * column_blocks + local_cols
        live_mask = (jnp.arange(MAXT, dtype=jnp.int32) < counts_flat[device]).astype(jnp.float32)
        blocks = values_flat[device].astype(jnp.float32)
        return (global_rows.astype(jnp.int32), global_cols.astype(jnp.int32), live_mask, blocks)
    projected = jnp.dot(features, weight, precision=highest, preferred_element_type=jnp.float32)
    scaled = (degree_scale[:, None] * projected).astype(jnp.bfloat16)
    source_blocks = scaled.astype(jnp.float32).reshape(node_blocks, TILE, F)

    def forward_step(totals, device):
        global_rows, global_cols, live_mask, blocks = placement(device)
        gathered = source_blocks[global_cols]
        products = jnp.einsum('tij,tjf->tif', blocks, gathered, precision=highest) * live_mask[:, None, None]
        return (totals.at[global_rows].add(products), None)
    device_list = jnp.arange(devices, dtype=jnp.int32)
    summed, ignored = lax.scan(forward_step, jnp.zeros((node_blocks, TILE, F), jnp.float32), device_list)
    summed = summed.reshape(nodes, F)
    preact = degree_scale[:, None] * summed + layer_bias[None, :]
    activations, slopes = gelu_pair(preact)
    delta = cotangent * slopes
    bias_grad = lax.optimization_barrier(jnp.sum(delta, axis=0)) * norm_factor
    delta_scaled = (degree_scale[:, None] * delta).astype(jnp.bfloat16)
    delta_blocks = delta_scaled.astype(jnp.float32).reshape(node_blocks, TILE, F)

    def backward_step(totals, device):
        global_rows, global_cols, live_mask, blocks = placement(device)
        gathered = delta_blocks[global_rows]
        products = jnp.einsum('tji,tjf->tif', blocks, gathered, precision=highest) * live_mask[:, None, None]
        return (totals.at[global_cols].add(products), None)
    back_summed, ignored = lax.scan(backward_step, jnp.zeros((node_blocks, TILE, F), jnp.float32), device_list)
    back_summed = back_summed.reshape(nodes, F)
    scaled_grad = degree_scale[:, None] * back_summed
    weight_grad = jnp.dot(features.T, scaled_grad, precision=highest, preferred_element_type=jnp.float32) * norm_factor
    feature_grad = jnp.dot(scaled_grad, weight.T, precision=highest, preferred_element_type=jnp.float32)
    return (activations, feature_grad, weight_grad, bias_grad)
```

```python
import functools
import math

import jax
import jax.numpy as jnp
from jax import lax
from jax.experimental import pallas as pl
from jax.experimental.pallas import tpu as pltpu
from jax.sharding import PartitionSpec as P

HIGHEST = lax.Precision.HIGHEST
MESH = pl.DeviceIdType.MESH
WIRE = jnp.bfloat16


def gelu_pair(values):
    argument = 0.7978845608028654 * (values + 0.044715 * values * values * values)
    tangent = jnp.tanh(argument)
    output = 0.5 * values * (1.0 + tangent)
    slopes = 0.5 * (1.0 + tangent) + 0.5 * values * (
        1.0 - tangent * tangent
    ) * 0.7978845608028654 * (1.0 + 3.0 * 0.044715 * values * values)
    return (output, slopes)


def repeat(count, body):
    if count <= 8:
        for index in range(count):
            body(index)
    else:
        lax.fori_loop(0, count, lambda index, carry: (body(index), carry)[1], 0)


def dot(a, b, **kw):
    return jnp.dot(a, b, preferred_element_type=jnp.float32, **kw)


def kernel(
    rows, cols, norm,
    inverse, features, weight, bias, degree, cotangent, tile_hbm,
    activation, feature_grad, weight_grad, bias_grad,
    tiles, dense, dense_t, gathered, x_all, x_t, part_send, part_recv, delta_all,
    back_f32, back_send, back_recv, w_part, w_row, w_col, w_out,
    tile_sem, g_send, g_recv, x_send, x_recv, p_send, p_recv, d_send, d_recv,
    b_send, b_recv, wa_send, wa_recv, wb_send, wb_recv, wc_send, wc_recv,
):
    own, width = features.shape
    slots, tile, _ = tile_hbm.shape
    sub = own // tile
    piece = width // rows
    me_r = lax.axis_index("row")
    me_c = lax.axis_index("col")

    def row_peer(step):
        return lax.rem(me_r + step + 1, rows)

    def col_peer(step):
        return lax.rem(me_c + step + 1, cols)

    def to_row(step, src, dst, send, recv):
        return pltpu.make_async_remote_copy(
            src_ref=src, dst_ref=dst, send_sem=send.at[step], recv_sem=recv.at[step],
            device_id=(row_peer(step), me_c), device_id_type=MESH,
        )

    def to_col(step, src, dst, send, recv):
        return pltpu.make_async_remote_copy(
            src_ref=src, dst_ref=dst, send_sem=send.at[step], recv_sem=recv.at[step],
            device_id=(me_r, col_peer(step)), device_id_type=MESH,
        )

    barrier = pltpu.get_barrier_semaphore()

    def greet_row(step):
        pl.semaphore_signal(barrier, inc=1, device_id=(row_peer(step), me_c), device_id_type=MESH)

    def greet_col(step):
        pl.semaphore_signal(barrier, inc=1, device_id=(me_r, col_peer(step)), device_id_type=MESH)

    repeat(cols - 1, greet_col)
    repeat(rows - 1, greet_row)
    tiles[slots] = jnp.zeros((tile, tile), tiles.dtype)
    tile_copy = pltpu.make_async_copy(tile_hbm, tiles.at[pl.ds(0, slots)], tile_sem)
    tile_copy.start()

    scale = jnp.broadcast_to(degree[...], (width, own)).T
    projected = dot(features[...], weight[...], precision=HIGHEST)
    gathered[me_c] = (scale * projected).astype(jnp.bfloat16)
    x_own = scale * features[...]
    x_all[me_c] = x_own

    pl.semaphore_wait(barrier, rows + cols - 2)

    def gather_copy(step):
        return to_col(step, gathered.at[me_c], gathered.at[me_c], g_send, g_recv)

    repeat(cols - 1, lambda step: gather_copy(step).start())

    tile_copy.wait()

    def place(u):
        for v in range(cols * sub):
            block = tiles[inverse[u * (cols * sub) + v]]
            dense[u, :, v * tile : (v + 1) * tile] = block

    repeat(rows * sub, place)
    repeat(cols - 1, lambda step: gather_copy(step).wait_recv())

    source = gathered[...].reshape(cols * own, width)

    def partial(block):
        left = dense[pl.ds(block * sub, sub)].reshape(own, cols * own)
        return dot(left, source)

    def part_copy(step):
        return to_row(step, part_send.at[step], part_recv.at[step], p_send, p_recv)

    def send_part(step):
        part_send[step] = partial(row_peer(step)).astype(WIRE)
        part_copy(step).start()

    repeat(rows - 1, send_part)

    def x_copy(step):
        return to_col(step, x_all.at[me_c], x_all.at[me_c], x_send, x_recv)

    repeat(cols - 1, lambda step: x_copy(step).start())
    own_part = partial(me_r)

    def flip(u):
        for v in range(cols * sub):
            block = dense[u, :, v * tile : (v + 1) * tile]
            dense_t[v * tile : (v + 1) * tile, pl.ds(pl.multiple_of(u * tile, tile), tile)] = block.T

    repeat(rows * sub, flip)

    repeat(rows - 1, lambda step: part_copy(step).wait_recv())
    summed = own_part + jnp.sum(part_recv[...].astype(jnp.float32), axis=0)
    preact = scale * summed + bias[...]
    output, slopes = gelu_pair(preact)
    delta = cotangent[...] * slopes
    delta_all[me_r] = (scale * delta).astype(jnp.bfloat16)

    def delta_copy(step):
        return to_row(step, delta_all.at[me_r], delta_all.at[me_r], d_send, d_recv)

    repeat(rows - 1, lambda step: delta_copy(step).start())
    activation[...] = output
    bias_part = jnp.sum(delta, axis=0, keepdims=True)
    w_part[:, piece:, :] = jnp.broadcast_to(bias_part[None], (rows, 8, width))

    repeat(cols - 1, lambda step: x_copy(step).wait_recv())
    for v in range(cols):
        x_t[:, v * own : (v + 1) * own] = x_all[v].T

    repeat(rows - 1, lambda step: delta_copy(step).wait_recv())
    back_f32[...] = dot(dense_t[...], delta_all[...].reshape(rows * own, width)).reshape(
        cols, own, width
    )

    def back_copy(step):
        return to_col(step, back_send.at[step], back_recv.at[step], b_send, b_recv)

    def send_back(step):
        back_send[step] = back_f32[col_peer(step)].astype(WIRE)
        back_copy(step).start()

    repeat(cols - 1, send_back)

    w_local = dot(x_t[...], back_f32[...].reshape(cols * own, width), precision=HIGHEST)
    w_part[:, :piece, :] = w_local.reshape(rows, piece, width)
    w_row[me_r] = w_part[me_r]

    def wa_copy(step):
        return to_row(step, w_part.at[row_peer(step)], w_row.at[me_r], wa_send, wa_recv)

    repeat(rows - 1, lambda step: wa_copy(step).start())
    repeat(rows - 1, lambda step: wa_copy(step).wait_recv())
    w_col[me_c] = jnp.sum(w_row[...], axis=0)

    def wb_copy(step):
        return to_col(step, w_col.at[me_c], w_col.at[me_c], wb_send, wb_recv)

    repeat(cols - 1, lambda step: wb_copy(step).start())

    repeat(cols - 1, lambda step: back_copy(step).wait_recv())
    back_sum = back_f32[me_c] + jnp.sum(back_recv[...].astype(jnp.float32), axis=0)
    feature_grad[...] = lax.dot_general(
        scale * back_sum, weight[...], (((1,), (1,)), ((), ())),
        precision=HIGHEST, preferred_element_type=jnp.float32,
    )

    repeat(cols - 1, lambda step: wb_copy(step).wait_recv())
    total = jnp.sum(w_col[...], axis=0) * norm
    w_out[me_r] = total[:piece]
    bias_grad[...] = total[piece : piece + 1]

    def wc_copy(step):
        return to_row(step, w_out.at[me_r], w_out.at[me_r], wc_send, wc_recv)

    repeat(rows - 1, lambda step: wc_copy(step).start())
    repeat(rows - 1, lambda step: wc_copy(step).wait_recv())
    weight_grad[...] = w_out[...].reshape(width, width)

    for copy in (gather_copy, x_copy, back_copy, wb_copy):
        repeat(cols - 1, lambda step, copy=copy: copy(step).wait_send())
    for copy in (part_copy, delta_copy, wa_copy, wc_copy):
        repeat(rows - 1, lambda step, copy=copy: copy(step).wait_send())


def local(
    features, weight, layer_bias, degree_scale, tile_values, tile_slots, tile_count, cotangent
):
    own, width = features.shape
    slots, tile = tile_values.shape[2:4]
    rows = lax.axis_size("row")
    cols = lax.axis_size("col")
    sub = own // tile
    places = rows * sub * cols * sub
    piece = width // rows
    norm = 1.0 / math.sqrt(own * rows * cols)

    order = jnp.arange(slots, dtype=jnp.int32)
    hit = (tile_slots[0, 0][None, :] == jnp.arange(places, dtype=jnp.int32)[:, None]) & (
        order < tile_count[0, 0]
    )[None, :]
    inverse = jnp.min(jnp.where(hit, order[None, :], slots), axis=1)

    f32, bf16 = jnp.float32, jnp.bfloat16
    vmem = pl.BlockSpec(memory_space=pltpu.VMEM)
    r1, c1 = (rows - 1,), (cols - 1,)
    dma = pltpu.SemaphoreType.DMA
    outs = pl.pallas_call(
        functools.partial(kernel, rows, cols, norm),
        out_shape=(
            jax.ShapeDtypeStruct((own, width), f32),
            jax.ShapeDtypeStruct((own, width), f32),
            jax.ShapeDtypeStruct((width, width), f32),
            jax.ShapeDtypeStruct((1, width), f32),
        ),
        in_specs=[
            pl.BlockSpec(memory_space=pltpu.SMEM), vmem, vmem, vmem, vmem, vmem,
            pl.BlockSpec(memory_space=pl.ANY),
        ],
        out_specs=(vmem, vmem, vmem, vmem),
        scratch_shapes=[
            pltpu.VMEM((slots + 1, tile, tile), bf16),
            pltpu.VMEM((rows * sub, tile, cols * own), bf16),
            pltpu.VMEM((cols * own, rows * own), bf16),
            pltpu.VMEM((cols, own, width), bf16),
            pltpu.VMEM((cols, own, width), f32),
            pltpu.VMEM((width, cols * own), f32),
            pltpu.VMEM((rows - 1, own, width), WIRE),
            pltpu.VMEM((rows - 1, own, width), WIRE),
            pltpu.VMEM((rows, own, width), bf16),
            pltpu.VMEM((cols, own, width), f32),
            pltpu.VMEM((cols - 1, own, width), WIRE),
            pltpu.VMEM((cols - 1, own, width), WIRE),
            pltpu.VMEM((rows, piece + 8, width), f32),
            pltpu.VMEM((rows, piece + 8, width), f32),
            pltpu.VMEM((cols, piece + 8, width), f32),
            pltpu.VMEM((rows, piece, width), f32),
            dma, dma(c1), dma(c1), dma(c1), dma(c1), dma(r1), dma(r1), dma(r1), dma(r1),
            dma(c1), dma(c1), dma(r1), dma(r1), dma(c1), dma(c1), dma(r1), dma(r1),
        ],
        compiler_params=pltpu.CompilerParams(collective_id=0, has_side_effects=True),
        name="graph_layer",
    )(
        inverse, features, weight, layer_bias.reshape(1, width), degree_scale.reshape(1, own),
        cotangent, tile_values.reshape(slots, tile, tile),
    )
    return (outs[0], outs[1], outs[2], outs[3].reshape(width))


def solution(mesh):
    return jax.shard_map(
        local,
        mesh=mesh,
        in_specs=(
            P(("row", "col"), None),
            P(),
            P(),
            P(("row", "col")),
            P("row", "col", None, None, None),
            P("row", "col", None),
            P("row", "col"),
            P(("row", "col"), None),
        ),
        out_specs=(P(("row", "col"), None), P(("row", "col"), None), P(), P()),
        check_vma=False,
    )
```

```python
import functools
import math

import jax
import jax.numpy as jnp
from jax import lax
from jax.experimental import pallas as pl
from jax.experimental.pallas import tpu as pltpu
from jax.sharding import PartitionSpec as P

HIGHEST = lax.Precision.HIGHEST
MESH = pl.DeviceIdType.MESH
WIRE = jnp.bfloat16


def gelu_pair(values):
    argument = 0.7978845608028654 * (values + 0.044715 * values * values * values)
    tangent = jnp.tanh(argument)
    output = 0.5 * values * (1.0 + tangent)
    slopes = 0.5 * (1.0 + tangent) + 0.5 * values * (
        1.0 - tangent * tangent
    ) * 0.7978845608028654 * (1.0 + 3.0 * 0.044715 * values * values)
    return (output, slopes)


def repeat(count, body):
    if count <= 8:
        for index in range(count):
            body(index)
    else:
        lax.fori_loop(0, count, lambda index, carry: (body(index), carry)[1], 0)


def dot(a, b, **kw):
    return jnp.dot(a, b, preferred_element_type=jnp.float32, **kw)


def kernel(
    rows, cols, norm,
    features_hbm, weight_hbm, bias_hbm, degree_hbm, cotangent_hbm, tile_hbm, slot_hbm, live,
    activation, feature_grad, weight_grad, bias_grad,
    features, weight, bias, degree, cotangent, slot_list, found, inverse,
    tiles, dense, dense_t, gathered, part_send, part_recv, delta_all,
    back_f32, back_send, back_recv, w_part, w_row, w_col, w_out,
    in_sem, tile_sem, found_sem, g_send, g_recv, p_send, p_recv, d_send, d_recv,
    b_send, b_recv, wa_send, wa_recv, wb_send, wb_recv, wc_send, wc_recv,
):
    own, width = features.shape
    slots, tile, _ = tile_hbm.shape
    sub = own // tile
    piece = width // cols
    places = found.shape[0]
    me_r = lax.axis_index("row")
    me_c = lax.axis_index("col")

    def row_peer(step):
        return lax.rem(me_r + step + 1, rows)

    def col_peer(step):
        return lax.rem(me_c + step + 1, cols)

    def to_row(step, src, dst, send, recv):
        return pltpu.make_async_remote_copy(
            src_ref=src, dst_ref=dst, send_sem=send.at[step], recv_sem=recv.at[step],
            device_id=(row_peer(step), me_c), device_id_type=MESH,
        )

    def to_col(step, src, dst, send, recv):
        return pltpu.make_async_remote_copy(
            src_ref=src, dst_ref=dst, send_sem=send.at[step], recv_sem=recv.at[step],
            device_id=(me_r, col_peer(step)), device_id_type=MESH,
        )

    barrier = pltpu.get_barrier_semaphore()

    def greet_row(step):
        pl.semaphore_signal(barrier, inc=1, device_id=(row_peer(step), me_c), device_id_type=MESH)

    def greet_col(step):
        pl.semaphore_signal(barrier, inc=1, device_id=(me_r, col_peer(step)), device_id_type=MESH)

    repeat(cols - 1, greet_col)
    repeat(rows - 1, greet_row)
    loads = [
        pltpu.make_async_copy(src, dst, in_sem.at[index])
        for index, (src, dst) in enumerate((
            (features_hbm, features), (degree_hbm, degree), (slot_hbm, slot_list),
            (weight_hbm, weight), (bias_hbm, bias), (cotangent_hbm, cotangent),
        ))
    ]
    for load in loads:
        load.start()
    tile_copy = pltpu.make_async_copy(tile_hbm, tiles.at[pl.ds(0, slots)], tile_sem)
    tile_copy.start()
    tiles[slots] = jnp.zeros((tile, tile), tiles.dtype)
    for load in loads[:3]:
        load.wait()

    scale = jnp.broadcast_to(degree[...], (width, own)).T
    gathered[me_c] = (scale * features[...]).astype(jnp.bfloat16)

    pl.semaphore_wait(barrier, rows + cols - 2)

    def gather_copy(step):
        return to_col(step, gathered.at[me_c], gathered.at[me_c], g_send, g_recv)

    repeat(cols - 1, lambda step: gather_copy(step).start())

    order = lax.broadcasted_iota(jnp.int32, (places, slots), 1)
    spot = lax.broadcasted_iota(jnp.int32, (places, slots), 0)
    hit = (slot_list[...] == spot) & (order < live[0, 0])
    nearest = jnp.min(jnp.where(hit, order, slots), axis=1, keepdims=True)
    found[...] = jnp.broadcast_to(nearest, found.shape)
    found_copy = pltpu.make_async_copy(found, inverse, found_sem)
    found_copy.start()
    for load in loads[3:]:
        load.wait()
    found_copy.wait()
    tile_copy.wait()

    def place(u):
        for v in range(cols * sub):
            block = tiles[inverse[u * (cols * sub) + v, 0]]
            dense[u, :, v * tile : (v + 1) * tile] = block

    repeat(rows * sub, place)
    repeat(cols - 1, lambda step: gather_copy(step).wait_recv())

    source = gathered[...].reshape(cols * own, width)

    def partial(block):
        left = dense[pl.ds(block * sub, sub)].reshape(own, cols * own)
        return dot(left, source)

    def part_copy(step):
        return to_row(step, part_send.at[step], part_recv.at[step], p_send, p_recv)

    def send_part(step):
        part_send[step] = partial(row_peer(step)).astype(WIRE)
        part_copy(step).start()

    repeat(rows - 1, send_part)
    own_part = partial(me_r)

    def flip(u):
        for v in range(cols * sub):
            block = dense[u, :, v * tile : (v + 1) * tile]
            dense_t[v * tile : (v + 1) * tile, pl.ds(pl.multiple_of(u * tile, tile), tile)] = block.T

    repeat(rows * sub, flip)

    repeat(rows - 1, lambda step: part_copy(step).wait_recv())
    aggregate = own_part + jnp.sum(part_recv[...].astype(jnp.float32), axis=0)
    summed = dot(aggregate, weight[...], precision=HIGHEST)
    preact = scale * summed + bias[...]
    output, slopes = gelu_pair(preact)
    delta = cotangent[...] * slopes
    delta_scaled = (scale * delta).astype(jnp.bfloat16)
    delta_all[me_r] = delta_scaled

    def delta_copy(step):
        return to_row(step, delta_all.at[me_r], delta_all.at[me_r], d_send, d_recv)

    repeat(rows - 1, lambda step: delta_copy(step).start())
    bias_part = jnp.sum(delta, axis=0, keepdims=True)
    w_local = dot(aggregate.T, delta_scaled.astype(jnp.float32), precision=HIGHEST)
    w_part[:, :piece, :] = w_local.reshape(cols, piece, width)
    w_part[:, piece:, :] = jnp.broadcast_to(bias_part[None], (cols, 8, width))

    def wa_copy(step):
        return to_col(step, w_part.at[col_peer(step)], w_col.at[me_c], wa_send, wa_recv)

    repeat(cols - 1, lambda step: wa_copy(step).start())
    w_col[me_c] = w_part[me_c]
    activation[...] = output
    repeat(cols - 1, lambda step: wa_copy(step).wait_recv())
    w_row[me_r] = jnp.sum(w_col[...], axis=0)

    def wb_copy(step):
        return to_row(step, w_row.at[me_r], w_row.at[me_r], wb_send, wb_recv)

    repeat(rows - 1, lambda step: wb_copy(step).start())

    repeat(rows - 1, lambda step: delta_copy(step).wait_recv())
    back_f32[...] = dot(dense_t[...], delta_all[...].reshape(rows * own, width)).reshape(
        cols, own, width
    )

    def back_copy(step):
        return to_col(step, back_send.at[step], back_recv.at[step], b_send, b_recv)

    def send_back(step):
        back_send[step] = back_f32[col_peer(step)].astype(WIRE)
        back_copy(step).start()

    repeat(cols - 1, send_back)

    repeat(rows - 1, lambda step: wb_copy(step).wait_recv())
    total = jnp.sum(w_row[...], axis=0) * norm
    w_out[me_c] = total[:piece]

    def wc_copy(step):
        return to_col(step, w_out.at[me_c], w_out.at[me_c], wc_send, wc_recv)

    repeat(cols - 1, lambda step: wc_copy(step).start())
    bias_grad[...] = total[piece : piece + 1]

    repeat(cols - 1, lambda step: back_copy(step).wait_recv())
    back_sum = back_f32[me_c] + jnp.sum(back_recv[...].astype(jnp.float32), axis=0)
    feature_grad[...] = lax.dot_general(
        scale * back_sum, weight[...], (((1,), (1,)), ((), ())),
        precision=HIGHEST, preferred_element_type=jnp.float32,
    )

    repeat(cols - 1, lambda step: wc_copy(step).wait_recv())
    weight_grad[...] = w_out[...].reshape(width, width)

    for copy in (gather_copy, back_copy, wa_copy, wc_copy):
        repeat(cols - 1, lambda step, copy=copy: copy(step).wait_send())
    for copy in (part_copy, delta_copy, wb_copy):
        repeat(rows - 1, lambda step, copy=copy: copy(step).wait_send())


def write_out(*refs):
    half = len(refs) // 2
    for source, target in zip(refs[:half], refs[half:]):
        target[...] = source[...]


def local(
    features, weight, layer_bias, degree_scale, tile_values, tile_slots, tile_count, cotangent
):
    own, width = features.shape
    slots, tile = tile_values.shape[2:4]
    rows = lax.axis_size("row")
    cols = lax.axis_size("col")
    sub = own // tile
    places = rows * sub * cols * sub
    piece = width // cols
    norm = 1.0 / math.sqrt(own * rows * cols)

    f32, bf16, i32 = jnp.float32, jnp.bfloat16, jnp.int32
    vmem = pl.BlockSpec(memory_space=pltpu.VMEM)
    hbm = pl.BlockSpec(memory_space=pl.ANY)
    r1, c1 = (rows - 1,), (cols - 1,)
    dma = pltpu.SemaphoreType.DMA
    out_shape = (
        jax.ShapeDtypeStruct((own, width), f32),
        jax.ShapeDtypeStruct((own, width), f32),
        jax.ShapeDtypeStruct((width, width), f32),
        jax.ShapeDtypeStruct((1, width), f32),
    )
    outs = pl.pallas_call(
        functools.partial(kernel, rows, cols, norm),
        out_shape=out_shape,
        in_specs=[hbm] * 7 + [pl.BlockSpec(memory_space=pltpu.SMEM)],
        out_specs=(vmem, vmem, vmem, vmem),
        scratch_shapes=[
            pltpu.VMEM((own, width), f32),
            pltpu.VMEM((width, width), f32),
            pltpu.VMEM((1, width), f32),
            pltpu.VMEM((1, own), f32),
            pltpu.VMEM((own, width), f32),
            pltpu.VMEM((1, slots), i32),
            pltpu.VMEM((places, 128), i32),
            pltpu.SMEM((places, 128), i32),
            pltpu.VMEM((slots + 1, tile, tile), bf16),
            pltpu.VMEM((rows * sub, tile, cols * own), bf16),
            pltpu.VMEM((cols * own, rows * own), bf16),
            pltpu.VMEM((cols, own, width), bf16),
            pltpu.VMEM((rows - 1, own, width), WIRE),
            pltpu.VMEM((rows - 1, own, width), WIRE),
            pltpu.VMEM((rows, own, width), bf16),
            pltpu.VMEM((cols, own, width), f32),
            pltpu.VMEM((cols - 1, own, width), WIRE),
            pltpu.VMEM((cols - 1, own, width), WIRE),
            pltpu.VMEM((cols, piece + 8, width), f32),
            pltpu.VMEM((rows, piece + 8, width), f32),
            pltpu.VMEM((cols, piece + 8, width), f32),
            pltpu.VMEM((cols, piece, width), f32),
            dma((6,)), dma, dma, dma(c1), dma(c1), dma(r1), dma(r1), dma(r1), dma(r1),
            dma(c1), dma(c1), dma(c1), dma(c1), dma(r1), dma(r1), dma(c1), dma(c1),
        ],
        compiler_params=pltpu.CompilerParams(collective_id=0, has_side_effects=True),
        name="graph_layer",
    )(
        features, weight, layer_bias.reshape(1, width), degree_scale.reshape(1, own),
        cotangent, tile_values.reshape(slots, tile, tile), tile_slots.reshape(1, slots),
        tile_count,
    )
    outs = pl.pallas_call(
        write_out,
        out_shape=out_shape,
        in_specs=[vmem] * 4,
        out_specs=(vmem, vmem, vmem, vmem),
        name="write_out",
    )(*outs)
    return (outs[0], outs[1], outs[2], outs[3].reshape(width))


def solution(mesh):
    return jax.shard_map(
        local,
        mesh=mesh,
        in_specs=(
            P(("row", "col"), None),
            P(),
            P(),
            P(("row", "col")),
            P("row", "col", None, None, None),
            P("row", "col", None),
            P("row", "col"),
            P(("row", "col"), None),
        ),
        out_specs=(P(("row", "col"), None), P(("row", "col"), None), P(), P()),
        check_vma=False,
    )
```

```python
import functools
import math

import jax
import jax.numpy as jnp
from jax import lax
from jax.experimental import pallas as pl
from jax.experimental.pallas import tpu as pltpu
from jax.sharding import PartitionSpec as P

HIGHEST = lax.Precision.HIGHEST
MESH = pl.DeviceIdType.MESH
WIRE = jnp.bfloat16


def gelu_pair(values):
    argument = 0.7978845608028654 * (values + 0.044715 * values * values * values)
    tangent = jnp.tanh(argument)
    output = 0.5 * values * (1.0 + tangent)
    slopes = 0.5 * (1.0 + tangent) + 0.5 * values * (
        1.0 - tangent * tangent
    ) * 0.7978845608028654 * (1.0 + 3.0 * 0.044715 * values * values)
    return (output, slopes)


def repeat(count, body):
    if count <= 8:
        for index in range(count):
            body(index)
    else:
        lax.fori_loop(0, count, lambda index, carry: (body(index), carry)[1], 0)


def dot(a, b, **kw):
    return jnp.dot(a, b, preferred_element_type=jnp.float32, **kw)


def kernel(
    rows, cols, norm,
    features_hbm, weight_hbm, bias_hbm, degree_hbm, cotangent_hbm, tile_hbm, slot_hbm, count_hbm,
    activation, feature_grad, weight_grad, bias_grad,
    features, weight, bias, degree, cotangent, slot_list, live, found, inverse,
    tiles, dense, dense_t, gathered, part_send, part_recv, delta_all,
    back_f32, back_send, back_recv, w_part, w_row, w_col, w_out,
    in_sem, tile_sem, found_sem, g_send, g_recv, p_send, p_recv, d_send, d_recv,
    b_send, b_recv, wa_send, wa_recv, wb_send, wb_recv, wc_send, wc_recv,
):
    own, width = features.shape
    slots, tile, _ = tile_hbm.shape
    sub = own // tile
    piece = width // cols
    places = found.shape[0]
    me_r = lax.axis_index("row")
    me_c = lax.axis_index("col")

    def row_peer(step):
        return lax.rem(me_r + step + 1, rows)

    def col_peer(step):
        return lax.rem(me_c + step + 1, cols)

    def to_row(step, src, dst, send, recv):
        return pltpu.make_async_remote_copy(
            src_ref=src, dst_ref=dst, send_sem=send.at[step], recv_sem=recv.at[step],
            device_id=(row_peer(step), me_c), device_id_type=MESH,
        )

    def to_col(step, src, dst, send, recv):
        return pltpu.make_async_remote_copy(
            src_ref=src, dst_ref=dst, send_sem=send.at[step], recv_sem=recv.at[step],
            device_id=(me_r, col_peer(step)), device_id_type=MESH,
        )

    barrier = pltpu.get_barrier_semaphore()

    def greet_row(step):
        pl.semaphore_signal(barrier, inc=1, device_id=(row_peer(step), me_c), device_id_type=MESH)

    def greet_col(step):
        pl.semaphore_signal(barrier, inc=1, device_id=(me_r, col_peer(step)), device_id_type=MESH)

    repeat(cols - 1, greet_col)
    repeat(rows - 1, greet_row)
    loads = [
        pltpu.make_async_copy(src, dst, in_sem.at[index])
        for index, (src, dst) in enumerate((
            (features_hbm, features), (degree_hbm, degree), (slot_hbm, slot_list),
            (count_hbm, live), (weight_hbm, weight), (bias_hbm, bias), (cotangent_hbm, cotangent),
        ))
    ]
    for load in loads:
        load.start()
    tile_copy = pltpu.make_async_copy(tile_hbm, tiles.at[pl.ds(0, slots)], tile_sem)
    tile_copy.start()
    tiles[slots] = jnp.zeros((tile, tile), tiles.dtype)
    for load in loads[:4]:
        load.wait()

    scale = jnp.broadcast_to(degree[...], (width, own)).T
    gathered[me_c] = (scale * features[...]).astype(jnp.bfloat16)

    pl.semaphore_wait(barrier, rows + cols - 2)

    def gather_copy(step):
        return to_col(step, gathered.at[me_c], gathered.at[me_c], g_send, g_recv)

    repeat(cols - 1, lambda step: gather_copy(step).start())

    order = lax.broadcasted_iota(jnp.int32, (places, slots), 1)
    spot = lax.broadcasted_iota(jnp.int32, (places, slots), 0)
    hit = (slot_list[...] == spot) & (order < live[...][:, None])
    nearest = jnp.min(jnp.where(hit, order, slots), axis=1, keepdims=True)
    found[...] = jnp.broadcast_to(nearest, found.shape)
    found_copy = pltpu.make_async_copy(found, inverse, found_sem)
    found_copy.start()
    for load in loads[4:]:
        load.wait()
    found_copy.wait()
    tile_copy.wait()

    def place(u):
        for v in range(cols * sub):
            block = tiles[inverse[u * (cols * sub) + v, 0]]
            dense[u, :, v * tile : (v + 1) * tile] = block

    repeat(rows * sub, place)
    repeat(cols - 1, lambda step: gather_copy(step).wait_recv())

    source = gathered[...].reshape(cols * own, width)

    def partial(block):
        left = dense[pl.ds(block * sub, sub)].reshape(own, cols * own)
        return dot(left, source)

    def part_copy(step):
        return to_row(step, part_send.at[step], part_recv.at[step], p_send, p_recv)

    def send_part(step):
        part_send[step] = partial(row_peer(step)).astype(WIRE)
        part_copy(step).start()

    repeat(rows - 1, send_part)
    own_part = partial(me_r)

    def flip(u):
        for v in range(cols * sub):
            block = dense[u, :, v * tile : (v + 1) * tile]
            dense_t[v * tile : (v + 1) * tile, pl.ds(pl.multiple_of(u * tile, tile), tile)] = block.T

    repeat(rows * sub, flip)

    repeat(rows - 1, lambda step: part_copy(step).wait_recv())
    aggregate = own_part + jnp.sum(part_recv[...].astype(jnp.float32), axis=0)
    summed = dot(aggregate, weight[...], precision=HIGHEST)
    preact = scale * summed + bias[...]
    output, slopes = gelu_pair(preact)
    delta = cotangent[...] * slopes
    delta_scaled = (scale * delta).astype(jnp.bfloat16)
    delta_all[me_r] = delta_scaled

    def delta_copy(step):
        return to_row(step, delta_all.at[me_r], delta_all.at[me_r], d_send, d_recv)

    repeat(rows - 1, lambda step: delta_copy(step).start())
    bias_part = jnp.sum(delta, axis=0, keepdims=True)
    w_local = dot(aggregate.T, delta_scaled.astype(jnp.float32), precision=HIGHEST)
    w_part[:, :piece, :] = w_local.reshape(cols, piece, width)
    w_part[:, piece:, :] = jnp.broadcast_to(bias_part[None], (cols, 8, width))

    def wa_copy(step):
        return to_col(step, w_part.at[col_peer(step)], w_col.at[me_c], wa_send, wa_recv)

    repeat(cols - 1, lambda step: wa_copy(step).start())
    w_col[me_c] = w_part[me_c]
    activation[...] = output
    repeat(cols - 1, lambda step: wa_copy(step).wait_recv())
    w_row[me_r] = jnp.sum(w_col[...], axis=0)

    def wb_copy(step):
        return to_row(step, w_row.at[me_r], w_row.at[me_r], wb_send, wb_recv)

    repeat(rows - 1, lambda step: wb_copy(step).start())

    repeat(rows - 1, lambda step: delta_copy(step).wait_recv())
    back_f32[...] = dot(dense_t[...], delta_all[...].reshape(rows * own, width)).reshape(
        cols, own, width
    )

    def back_copy(step):
        return to_col(step, back_send.at[step], back_recv.at[step], b_send, b_recv)

    def send_back(step):
        back_send[step] = back_f32[col_peer(step)].astype(WIRE)
        back_copy(step).start()

    repeat(cols - 1, send_back)

    repeat(rows - 1, lambda step: wb_copy(step).wait_recv())
    total = jnp.sum(w_row[...], axis=0) * norm
    w_out[me_c] = total[:piece]

    def wc_copy(step):
        return to_col(step, w_out.at[me_c], w_out.at[me_c], wc_send, wc_recv)

    repeat(cols - 1, lambda step: wc_copy(step).start())
    bias_grad[...] = total[piece : piece + 1]

    repeat(cols - 1, lambda step: back_copy(step).wait_recv())
    back_sum = back_f32[me_c] + jnp.sum(back_recv[...].astype(jnp.float32), axis=0)
    feature_grad[...] = lax.dot_general(
        scale * back_sum, weight[...], (((1,), (1,)), ((), ())),
        precision=HIGHEST, preferred_element_type=jnp.float32,
    )

    repeat(cols - 1, lambda step: wc_copy(step).wait_recv())
    weight_grad[...] = w_out[...].reshape(width, width)

    for copy in (gather_copy, back_copy, wa_copy, wc_copy):
        repeat(cols - 1, lambda step, copy=copy: copy(step).wait_send())
    for copy in (part_copy, delta_copy, wb_copy):
        repeat(rows - 1, lambda step, copy=copy: copy(step).wait_send())


def write_out(*refs):
    *refs, sem = refs
    half = len(refs) // 2
    copies = [
        pltpu.make_async_copy(refs[index], refs[half + index], sem.at[index])
        for index in range(half)
    ]
    for copy in copies:
        copy.start()
    for copy in copies:
        copy.wait()


def local(
    features, weight, layer_bias, degree_scale, tile_values, tile_slots, tile_count, cotangent
):
    own, width = features.shape
    slots, tile = tile_values.shape[2:4]
    rows = lax.axis_size("row")
    cols = lax.axis_size("col")
    sub = own // tile
    places = rows * sub * cols * sub
    piece = width // cols
    norm = 1.0 / math.sqrt(own * rows * cols)

    f32, bf16, i32 = jnp.float32, jnp.bfloat16, jnp.int32
    vmem = pl.BlockSpec(memory_space=pltpu.VMEM)
    r1, c1 = (rows - 1,), (cols - 1,)
    dma = pltpu.SemaphoreType.DMA
    out_shape = (
        jax.ShapeDtypeStruct((own, width), f32),
        jax.ShapeDtypeStruct((own, width), f32),
        jax.ShapeDtypeStruct((width, width), f32),
        jax.ShapeDtypeStruct((1, width), f32),
    )
    outs = pl.pallas_call(
        functools.partial(kernel, rows, cols, norm),
        out_shape=tuple(pltpu.VMEM(out.shape, out.dtype) for out in out_shape),
        in_specs=[pl.BlockSpec(memory_space=pltpu.HBM)] * 8,
        out_specs=(vmem, vmem, vmem, vmem),
        scratch_shapes=[
            pltpu.VMEM((own, width), f32),
            pltpu.VMEM((width, width), f32),
            pltpu.VMEM((1, width), f32),
            pltpu.VMEM((1, own), f32),
            pltpu.VMEM((own, width), f32),
            pltpu.VMEM((1, slots), i32),
            pltpu.VMEM((1,), i32),
            pltpu.VMEM((places, 128), i32),
            pltpu.SMEM((places, 128), i32),
            pltpu.VMEM((slots + 1, tile, tile), bf16),
            pltpu.VMEM((rows * sub, tile, cols * own), bf16),
            pltpu.VMEM((cols * own, rows * own), bf16),
            pltpu.VMEM((cols, own, width), bf16),
            pltpu.VMEM((rows - 1, own, width), WIRE),
            pltpu.VMEM((rows - 1, own, width), WIRE),
            pltpu.VMEM((rows, own, width), bf16),
            pltpu.VMEM((cols, own, width), f32),
            pltpu.VMEM((cols - 1, own, width), WIRE),
            pltpu.VMEM((cols - 1, own, width), WIRE),
            pltpu.VMEM((cols, piece + 8, width), f32),
            pltpu.VMEM((rows, piece + 8, width), f32),
            pltpu.VMEM((cols, piece + 8, width), f32),
            pltpu.VMEM((cols, piece, width), f32),
            dma((7,)), dma, dma, dma(c1), dma(c1), dma(r1), dma(r1), dma(r1), dma(r1),
            dma(c1), dma(c1), dma(c1), dma(c1), dma(r1), dma(r1), dma(c1), dma(c1),
        ],
        compiler_params=pltpu.CompilerParams(collective_id=0, has_side_effects=True),
        name="graph_layer",
    )(
        features, weight, layer_bias.reshape(1, width), degree_scale.reshape(1, own),
        cotangent, tile_values.reshape(slots, tile, tile), tile_slots.reshape(1, slots),
        tile_count.reshape(1),
    )
    outs = pl.pallas_call(
        write_out,
        out_shape=out_shape,
        in_specs=[vmem] * 4,
        out_specs=[pl.BlockSpec(memory_space=pltpu.HBM)] * 4,
        scratch_shapes=[dma((4,))],
        name="write_out",
    )(*[pltpu.with_memory_space_constraint(out, pltpu.VMEM) for out in outs])
    return (outs[0], outs[1], outs[2], outs[3].reshape(width))


def solution(mesh):
    return jax.shard_map(
        local,
        mesh=mesh,
        in_specs=(
            P(("row", "col"), None),
            P(),
            P(),
            P(("row", "col")),
            P("row", "col", None, None, None),
            P("row", "col", None),
            P("row", "col"),
            P(("row", "col"), None),
        ),
        out_specs=(P(("row", "col"), None), P(("row", "col"), None), P(), P()),
        check_vma=False,
    )
```

```python
import functools
import math

import jax
import jax.numpy as jnp
from jax import lax
from jax.experimental import pallas as pl
from jax.experimental.pallas import tpu as pltpu
from jax.sharding import PartitionSpec as P

MESH = pl.DeviceIdType.MESH
WIRE = jnp.bfloat16


def gelu_pair(values):
    argument = 0.7978845608028654 * (values + 0.044715 * values * values * values)
    tangent = jnp.tanh(argument)
    output = 0.5 * values * (1.0 + tangent)
    slopes = 0.5 * (1.0 + tangent) + 0.5 * values * (
        1.0 - tangent * tangent
    ) * 0.7978845608028654 * (1.0 + 3.0 * 0.044715 * values * values)
    return (output, slopes)


def repeat(count, body):
    if count <= 8:
        for index in range(count):
            body(index)
    else:
        lax.fori_loop(0, count, lambda index, carry: (body(index), carry)[1], 0)


def dot(a, b, **kw):
    return jnp.dot(a, b, preferred_element_type=jnp.float32, **kw)


def halves(values):
    high = values.astype(jnp.bfloat16)
    return high, (values - high.astype(jnp.float32)).astype(jnp.bfloat16)


def split_dot(values, stacked):
    high, low = halves(values)
    return dot(jnp.concatenate([high, low, high], axis=1), stacked)


def kernel(
    rows, cols, norm,
    features_hbm, weight_hbm, bias_hbm, degree_hbm, cotangent_hbm, tile_hbm, slot_hbm, count_hbm,
    activation, feature_grad, weight_grad, bias_grad,
    features, weight, bias, degree, cotangent, slot_list, live, found, inverse,
    tiles, dense, dense_t, gathered, part_send, part_recv, delta_all,
    weight_split, turned_split,
    back_f32, back_send, back_recv, w_part, w_row, w_col, w_out,
    in_sem, tile_sem, found_sem, g_send, g_recv, p_send, p_recv, d_send, d_recv,
    b_send, b_recv, wa_send, wa_recv, wb_send, wb_recv, wc_send, wc_recv,
):
    own, width = features.shape
    slots, tile, _ = tile_hbm.shape
    sub = own // tile
    piece = width // cols
    places = found.shape[0]
    me_r = lax.axis_index("row")
    me_c = lax.axis_index("col")

    def row_peer(step):
        return lax.rem(me_r + step + 1, rows)

    def col_peer(step):
        return lax.rem(me_c + step + 1, cols)

    def to_row(step, src, dst, send, recv):
        return pltpu.make_async_remote_copy(
            src_ref=src, dst_ref=dst, send_sem=send.at[step], recv_sem=recv.at[step],
            device_id=(row_peer(step), me_c), device_id_type=MESH,
        )

    def to_col(step, src, dst, send, recv):
        return pltpu.make_async_remote_copy(
            src_ref=src, dst_ref=dst, send_sem=send.at[step], recv_sem=recv.at[step],
            device_id=(me_r, col_peer(step)), device_id_type=MESH,
        )

    barrier = pltpu.get_barrier_semaphore()

    def greet_row(step):
        pl.semaphore_signal(barrier, inc=1, device_id=(row_peer(step), me_c), device_id_type=MESH)

    def greet_col(step):
        pl.semaphore_signal(barrier, inc=1, device_id=(me_r, col_peer(step)), device_id_type=MESH)

    repeat(cols - 1, greet_col)
    repeat(rows - 1, greet_row)
    loads = [
        pltpu.make_async_copy(src, dst, in_sem.at[index])
        for index, (src, dst) in enumerate((
            (features_hbm, features), (degree_hbm, degree), (slot_hbm, slot_list),
            (count_hbm, live), (weight_hbm, weight), (bias_hbm, bias), (cotangent_hbm, cotangent),
        ))
    ]
    for load in loads:
        load.start()
    tile_copy = pltpu.make_async_copy(tile_hbm, tiles.at[pl.ds(0, slots)], tile_sem)
    tile_copy.start()
    tiles[slots] = jnp.zeros((tile, tile), tiles.dtype)
    for load in loads[:4]:
        load.wait()

    scale = jnp.broadcast_to(degree[...], (width, own)).T
    gathered[me_c] = (scale * features[...]).astype(jnp.bfloat16)

    pl.semaphore_wait(barrier, rows + cols - 2)

    def gather_copy(step):
        return to_col(step, gathered.at[me_c], gathered.at[me_c], g_send, g_recv)

    repeat(cols - 1, lambda step: gather_copy(step).start())

    order = lax.broadcasted_iota(jnp.int32, (places, slots), 1)
    spot = lax.broadcasted_iota(jnp.int32, (places, slots), 0)
    hit = (slot_list[...] == spot) & (order < live[...][:, None])
    nearest = jnp.min(jnp.where(hit, order, slots), axis=1, keepdims=True)
    found[...] = jnp.broadcast_to(nearest, found.shape)
    found_copy = pltpu.make_async_copy(found, inverse, found_sem)
    found_copy.start()
    for load in loads[4:]:
        load.wait()
    for matrix, stacked in ((weight[...], weight_split), (weight[...].T, turned_split)):
        high, low = halves(matrix)
        stacked[:width] = high
        stacked[width : 2 * width] = high
        stacked[2 * width :] = low
    found_copy.wait()
    tile_copy.wait()

    def place(u):
        for v in range(cols * sub):
            block = tiles[inverse[u * (cols * sub) + v, 0]]
            dense[u, :, v * tile : (v + 1) * tile] = block

    repeat(rows * sub, place)
    repeat(cols - 1, lambda step: gather_copy(step).wait_recv())

    source = gathered[...].reshape(cols * own, width)

    def partial(block):
        left = dense[pl.ds(block * sub, sub)].reshape(own, cols * own)
        return dot(left, source)

    def part_copy(step):
        return to_row(step, part_send.at[step], part_recv.at[step], p_send, p_recv)

    def send_part(step):
        part_send[step] = partial(row_peer(step)).astype(WIRE)
        part_copy(step).start()

    repeat(rows - 1, send_part)
    own_part = partial(me_r)

    def flip(u):
        for v in range(cols * sub):
            block = dense[u, :, v * tile : (v + 1) * tile]
            dense_t[v * tile : (v + 1) * tile, pl.ds(pl.multiple_of(u * tile, tile), tile)] = block.T

    repeat(rows * sub, flip)

    repeat(rows - 1, lambda step: part_copy(step).wait_recv())
    aggregate = own_part + jnp.sum(part_recv[...].astype(jnp.float32), axis=0)
    summed = split_dot(aggregate, weight_split[...])
    preact = scale * summed + bias[...]
    output, slopes = gelu_pair(preact)
    delta = cotangent[...] * slopes
    delta_scaled = (scale * delta).astype(jnp.bfloat16)
    delta_all[me_r] = delta_scaled

    def delta_copy(step):
        return to_row(step, delta_all.at[me_r], delta_all.at[me_r], d_send, d_recv)

    repeat(rows - 1, lambda step: delta_copy(step).start())
    bias_part = jnp.sum(delta, axis=0, keepdims=True)
    high, low = halves(aggregate.T)
    w_local = dot(high, delta_scaled) + dot(low, delta_scaled)
    w_part[:, :piece, :] = w_local.reshape(cols, piece, width)
    w_part[:, piece:, :] = jnp.broadcast_to(bias_part[None], (cols, 8, width))

    def wa_copy(step):
        return to_col(step, w_part.at[col_peer(step)], w_col.at[me_c], wa_send, wa_recv)

    repeat(cols - 1, lambda step: wa_copy(step).start())
    w_col[me_c] = w_part[me_c]
    activation[...] = output
    repeat(cols - 1, lambda step: wa_copy(step).wait_recv())
    reduced = jnp.sum(w_col[...], axis=0)
    w_row[me_r, :piece, :] = reduced[:piece].astype(WIRE)
    w_row[me_r, piece:, :] = jnp.broadcast_to(reduced[piece : piece + 1], (16, width)).astype(WIRE)

    def wb_copy(step):
        return to_row(step, w_row.at[me_r], w_row.at[me_r], wb_send, wb_recv)

    repeat(rows - 1, lambda step: wb_copy(step).start())

    repeat(rows - 1, lambda step: delta_copy(step).wait_recv())
    back_f32[...] = dot(dense_t[...], delta_all[...].reshape(rows * own, width)).reshape(
        cols, own, width
    )

    def back_copy(step):
        return to_col(step, back_send.at[step], back_recv.at[step], b_send, b_recv)

    def send_back(step):
        back_send[step] = back_f32[col_peer(step)].astype(WIRE)
        back_copy(step).start()

    repeat(cols - 1, send_back)

    repeat(rows - 1, lambda step: wb_copy(step).wait_recv())
    total = jnp.sum(w_row[...].astype(jnp.float32), axis=0) * norm
    w_out[me_c] = total[:piece]

    def wc_copy(step):
        return to_col(step, w_out.at[me_c], w_out.at[me_c], wc_send, wc_recv)

    repeat(cols - 1, lambda step: wc_copy(step).start())
    bias_grad[...] = total[piece : piece + 1]

    repeat(cols - 1, lambda step: back_copy(step).wait_recv())
    back_sum = back_f32[me_c] + jnp.sum(back_recv[...].astype(jnp.float32), axis=0)
    feature_grad[...] = split_dot(scale * back_sum, turned_split[...])

    repeat(cols - 1, lambda step: wc_copy(step).wait_recv())
    weight_grad[...] = w_out[...].reshape(width, width)

    for copy in (gather_copy, back_copy, wa_copy, wc_copy):
        repeat(cols - 1, lambda step, copy=copy: copy(step).wait_send())
    for copy in (part_copy, delta_copy, wb_copy):
        repeat(rows - 1, lambda step, copy=copy: copy(step).wait_send())


def write_out(*refs):
    *refs, sem = refs
    half = len(refs) // 2
    copies = [
        pltpu.make_async_copy(refs[index], refs[half + index], sem.at[index])
        for index in range(half)
    ]
    for copy in copies:
        copy.start()
    for copy in copies:
        copy.wait()


def local(
    features, weight, layer_bias, degree_scale, tile_values, tile_slots, tile_count, cotangent
):
    own, width = features.shape
    slots, tile = tile_values.shape[2:4]
    rows = lax.axis_size("row")
    cols = lax.axis_size("col")
    sub = own // tile
    places = rows * sub * cols * sub
    piece = width // cols
    norm = 1.0 / math.sqrt(own * rows * cols)

    f32, bf16, i32 = jnp.float32, jnp.bfloat16, jnp.int32
    vmem = pl.BlockSpec(memory_space=pltpu.VMEM)
    r1, c1 = (rows - 1,), (cols - 1,)
    dma = pltpu.SemaphoreType.DMA
    out_shape = (
        jax.ShapeDtypeStruct((own, width), f32),
        jax.ShapeDtypeStruct((own, width), f32),
        jax.ShapeDtypeStruct((width, width), f32),
        jax.ShapeDtypeStruct((1, width), f32),
    )
    outs = pl.pallas_call(
        functools.partial(kernel, rows, cols, norm),
        out_shape=tuple(pltpu.VMEM(out.shape, out.dtype) for out in out_shape),
        in_specs=[pl.BlockSpec(memory_space=pltpu.HBM)] * 8,
        out_specs=(vmem, vmem, vmem, vmem),
        scratch_shapes=[
            pltpu.VMEM((own, width), f32),
            pltpu.VMEM((width, width), f32),
            pltpu.VMEM((1, width), f32),
            pltpu.VMEM((1, own), f32),
            pltpu.VMEM((own, width), f32),
            pltpu.VMEM((1, slots), i32),
            pltpu.VMEM((1,), i32),
            pltpu.VMEM((places, 128), i32),
            pltpu.SMEM((places, 128), i32),
            pltpu.VMEM((slots + 1, tile, tile), bf16),
            pltpu.VMEM((rows * sub, tile, cols * own), bf16),
            pltpu.VMEM((cols * own, rows * own), bf16),
            pltpu.VMEM((cols, own, width), bf16),
            pltpu.VMEM((rows - 1, own, width), WIRE),
            pltpu.VMEM((rows - 1, own, width), WIRE),
            pltpu.VMEM((rows, own, width), bf16),
            pltpu.VMEM((3 * width, width), bf16),
            pltpu.VMEM((3 * width, width), bf16),
            pltpu.VMEM((cols, own, width), f32),
            pltpu.VMEM((cols - 1, own, width), WIRE),
            pltpu.VMEM((cols - 1, own, width), WIRE),
            pltpu.VMEM((cols, piece + 8, width), f32),
            pltpu.VMEM((rows, piece + 16, width), WIRE),
            pltpu.VMEM((cols, piece + 8, width), f32),
            pltpu.VMEM((cols, piece, width), f32),
            dma((7,)), dma, dma, dma(c1), dma(c1), dma(r1), dma(r1), dma(r1), dma(r1),
            dma(c1), dma(c1), dma(c1), dma(c1), dma(r1), dma(r1), dma(c1), dma(c1),
        ],
        compiler_params=pltpu.CompilerParams(collective_id=0, has_side_effects=True),
        name="graph_layer",
    )(
        features, weight, layer_bias.reshape(1, width), degree_scale.reshape(1, own),
        cotangent, tile_values.reshape(slots, tile, tile), tile_slots.reshape(1, slots),
        tile_count.reshape(1),
    )
    outs = pl.pallas_call(
        write_out,
        out_shape=out_shape,
        in_specs=[vmem] * 4,
        out_specs=[pl.BlockSpec(memory_space=pltpu.HBM)] * 4,
        scratch_shapes=[dma((4,))],
        name="write_out",
    )(*[pltpu.with_memory_space_constraint(out, pltpu.VMEM) for out in outs])
    return (outs[0], outs[1], outs[2], outs[3].reshape(width))


def solution(mesh):
    return jax.shard_map(
        local,
        mesh=mesh,
        in_specs=(
            P(("row", "col"), None),
            P(),
            P(),
            P(("row", "col")),
            P("row", "col", None, None, None),
            P("row", "col", None),
            P("row", "col"),
            P(("row", "col"), None),
        ),
        out_specs=(P(("row", "col"), None), P(("row", "col"), None), P(), P()),
        check_vma=False,
    )
```

```python
import functools
import math

import jax
import jax.numpy as jnp
from jax import lax
from jax.experimental import pallas as pl
from jax.experimental.pallas import tpu as pltpu
from jax.sharding import PartitionSpec as P

MESH = pl.DeviceIdType.MESH
WIRE = jnp.bfloat16


def gelu_pair(values):
    argument = 0.7978845608028654 * (values + 0.044715 * values * values * values)
    tangent = jnp.tanh(argument)
    output = 0.5 * values * (1.0 + tangent)
    slopes = 0.5 * (1.0 + tangent) + 0.5 * values * (
        1.0 - tangent * tangent
    ) * 0.7978845608028654 * (1.0 + 3.0 * 0.044715 * values * values)
    return (output, slopes)


def repeat(count, body):
    if count <= 8:
        for index in range(count):
            body(index)
    else:
        lax.fori_loop(0, count, lambda index, carry: (body(index), carry)[1], 0)


def dot(a, b, **kw):
    return jnp.dot(a, b, preferred_element_type=jnp.float32, **kw)


def halves(values):
    high = values.astype(jnp.bfloat16)
    return high, (values - high.astype(jnp.float32)).astype(jnp.bfloat16)


def split_dot(values, stacked):
    high, low = halves(values)
    return dot(jnp.concatenate([high, low, high], axis=1), stacked)


def kernel(
    rows, cols, norm,
    features_hbm, weight_hbm, bias_hbm, degree_hbm, cotangent_hbm, tile_hbm, slot_hbm, count_hbm,
    activation, feature_grad, weight_grad, bias_grad,
    features, weight, bias, degree, cotangent, slot_list, live, found, inverse,
    tiles, dense, dense_t, gathered, part_send, part_recv, delta_all,
    weight_split, turned_split,
    back_f32, back_send, back_recv, w_part, w_row, w_col, w_out,
    in_sem, tile_sem, found_sem, g_send, g_recv, p_send, p_recv, d_send, d_recv,
    b_send, b_recv, wa_send, wa_recv, wb_send, wb_recv, wc_send, wc_recv,
):
    own, width = features.shape
    slots, tile, _ = tile_hbm.shape
    sub = own // tile
    piece = width // cols
    places = found.shape[0]
    me_r = lax.axis_index("row")
    me_c = lax.axis_index("col")

    def row_peer(step):
        return lax.rem(me_r + step + 1, rows)

    def col_peer(step):
        return lax.rem(me_c + step + 1, cols)

    def row_order(turn):
        other = rows - 1 - turn
        peer, bit = 0, 1
        while bit < rows:
            flipped = lax.rem(lax.div(me_r, jnp.int32(bit)) + other // bit, 2)
            peer, bit = peer + bit * flipped, bit * 2
        return lax.rem(peer - me_r - 1 + rows, rows)

    def col_order(turn):
        down = cols - 1 - turn
        down = down - lax.div(me_c - down + cols, cols)
        up = turn + lax.div(turn - me_c + cols, cols)
        high = lax.div(me_c * 2, cols)
        peer = high * up + (1 - high) * down
        return lax.rem(peer - me_c - 1 + cols, cols)

    def to_row(step, src, dst, send, recv):
        return pltpu.make_async_remote_copy(
            src_ref=src, dst_ref=dst, send_sem=send.at[step], recv_sem=recv.at[step],
            device_id=(row_peer(step), me_c), device_id_type=MESH,
        )

    def to_col(step, src, dst, send, recv):
        return pltpu.make_async_remote_copy(
            src_ref=src, dst_ref=dst, send_sem=send.at[step], recv_sem=recv.at[step],
            device_id=(me_r, col_peer(step)), device_id_type=MESH,
        )

    barrier = pltpu.get_barrier_semaphore()

    def greet_row(step):
        pl.semaphore_signal(barrier, inc=1, device_id=(row_peer(step), me_c), device_id_type=MESH)

    def greet_col(step):
        pl.semaphore_signal(barrier, inc=1, device_id=(me_r, col_peer(step)), device_id_type=MESH)

    repeat(cols - 1, greet_col)
    repeat(rows - 1, greet_row)
    loads = [
        pltpu.make_async_copy(src, dst, in_sem.at[index])
        for index, (src, dst) in enumerate((
            (features_hbm, features), (degree_hbm, degree), (slot_hbm, slot_list),
            (count_hbm, live), (weight_hbm, weight), (bias_hbm, bias), (cotangent_hbm, cotangent),
        ))
    ]
    for load in loads:
        load.start()
    tile_copy = pltpu.make_async_copy(tile_hbm, tiles.at[pl.ds(0, slots)], tile_sem)
    tile_copy.start()
    tiles[slots] = jnp.zeros((tile, tile), tiles.dtype)
    for load in loads[:4]:
        load.wait()

    scale = jnp.broadcast_to(degree[...], (width, own)).T
    gathered[me_c] = (scale * features[...]).astype(jnp.bfloat16)

    pl.semaphore_wait(barrier, rows + cols - 2)

    def gather_copy(step):
        return to_col(step, gathered.at[me_c], gathered.at[me_c], g_send, g_recv)

    repeat(cols - 1, lambda turn: gather_copy(col_order(turn)).start())

    order = lax.broadcasted_iota(jnp.int32, (places, slots), 1)
    spot = lax.broadcasted_iota(jnp.int32, (places, slots), 0)
    hit = (slot_list[...] == spot) & (order < live[...][:, None])
    nearest = jnp.min(jnp.where(hit, order, slots), axis=1, keepdims=True)
    found[...] = jnp.broadcast_to(nearest, found.shape)
    found_copy = pltpu.make_async_copy(found, inverse, found_sem)
    found_copy.start()
    for load in loads[4:]:
        load.wait()
    for matrix, stacked in ((weight[...], weight_split), (weight[...].T, turned_split)):
        high, low = halves(matrix)
        stacked[:width] = high
        stacked[width : 2 * width] = high
        stacked[2 * width :] = low
    found_copy.wait()
    tile_copy.wait()

    def place(u):
        for v in range(cols * sub):
            block = tiles[inverse[u * (cols * sub) + v, 0]]
            dense[u, :, v * tile : (v + 1) * tile] = block

    repeat(rows * sub, place)
    repeat(cols - 1, lambda step: gather_copy(step).wait_recv())

    source = gathered[...].reshape(cols * own, width)

    def partial(block):
        left = dense[pl.ds(block * sub, sub)].reshape(own, cols * own)
        return dot(left, source)

    def part_copy(step):
        return to_row(step, part_send.at[step], part_recv.at[step], p_send, p_recv)

    def send_part(step):
        part_send[step] = partial(row_peer(step)).astype(WIRE)
        part_copy(step).start()

    repeat(rows - 1, lambda turn: send_part(row_order(turn)))
    own_part = partial(me_r)

    def flip(u):
        for v in range(cols * sub):
            block = dense[u, :, v * tile : (v + 1) * tile]
            dense_t[v * tile : (v + 1) * tile, pl.ds(pl.multiple_of(u * tile, tile), tile)] = block.T

    repeat(rows * sub, flip)

    repeat(rows - 1, lambda step: part_copy(step).wait_recv())
    aggregate = own_part + jnp.sum(part_recv[...].astype(jnp.float32), axis=0)
    summed = split_dot(aggregate, weight_split[...])
    preact = scale * summed + bias[...]
    output, slopes = gelu_pair(preact)
    delta = cotangent[...] * slopes
    delta_scaled = (scale * delta).astype(jnp.bfloat16)
    delta_all[me_r] = delta_scaled

    def delta_copy(step):
        return to_row(step, delta_all.at[me_r], delta_all.at[me_r], d_send, d_recv)

    repeat(rows - 1, lambda turn: delta_copy(row_order(turn)).start())
    bias_part = jnp.sum(delta, axis=0, keepdims=True)
    high, low = halves(aggregate.T)
    w_local = dot(high, delta_scaled) + dot(low, delta_scaled)
    w_part[:, :piece, :] = w_local.reshape(cols, piece, width)
    w_part[:, piece:, :] = jnp.broadcast_to(bias_part[None], (cols, 8, width))

    def wa_copy(step):
        return to_col(step, w_part.at[col_peer(step)], w_col.at[me_c], wa_send, wa_recv)

    repeat(cols - 1, lambda turn: wa_copy(col_order(turn)).start())
    w_col[me_c] = w_part[me_c]
    activation[...] = output
    repeat(cols - 1, lambda step: wa_copy(step).wait_recv())
    reduced = jnp.sum(w_col[...], axis=0)
    w_row[me_r, :piece, :] = reduced[:piece].astype(WIRE)
    w_row[me_r, piece:, :] = jnp.broadcast_to(reduced[piece : piece + 1], (16, width)).astype(WIRE)

    def wb_copy(step):
        return to_row(step, w_row.at[me_r], w_row.at[me_r], wb_send, wb_recv)

    repeat(rows - 1, lambda turn: wb_copy(row_order(turn)).start())

    repeat(rows - 1, lambda step: delta_copy(step).wait_recv())
    back_f32[...] = dot(dense_t[...], delta_all[...].reshape(rows * own, width)).reshape(
        cols, own, width
    )

    def back_copy(step):
        return to_col(step, back_send.at[step], back_recv.at[step], b_send, b_recv)

    def send_back(step):
        back_send[step] = back_f32[col_peer(step)].astype(WIRE)
        back_copy(step).start()

    repeat(cols - 1, lambda turn: send_back(col_order(turn)))

    repeat(rows - 1, lambda step: wb_copy(step).wait_recv())
    total = jnp.sum(w_row[...].astype(jnp.float32), axis=0) * norm
    w_out[me_c] = total[:piece]

    def wc_copy(step):
        return to_col(step, w_out.at[me_c], w_out.at[me_c], wc_send, wc_recv)

    repeat(cols - 1, lambda turn: wc_copy(col_order(turn)).start())
    bias_grad[...] = total[piece : piece + 1]

    repeat(cols - 1, lambda step: back_copy(step).wait_recv())
    back_sum = back_f32[me_c] + jnp.sum(back_recv[...].astype(jnp.float32), axis=0)
    feature_grad[...] = split_dot(scale * back_sum, turned_split[...])

    repeat(cols - 1, lambda step: wc_copy(step).wait_recv())
    weight_grad[...] = w_out[...].reshape(width, width)

    for copy in (gather_copy, back_copy, wa_copy, wc_copy):
        repeat(cols - 1, lambda step, copy=copy: copy(step).wait_send())
    for copy in (part_copy, delta_copy, wb_copy):
        repeat(rows - 1, lambda step, copy=copy: copy(step).wait_send())


def write_out(*refs):
    *refs, sem = refs
    half = len(refs) // 2
    copies = [
        pltpu.make_async_copy(refs[index], refs[half + index], sem.at[index])
        for index in range(half)
    ]
    for copy in copies:
        copy.start()
    for copy in copies:
        copy.wait()


def local(
    features, weight, layer_bias, degree_scale, tile_values, tile_slots, tile_count, cotangent
):
    own, width = features.shape
    slots, tile = tile_values.shape[2:4]
    rows = lax.axis_size("row")
    cols = lax.axis_size("col")
    sub = own // tile
    places = rows * sub * cols * sub
    piece = width // cols
    norm = 1.0 / math.sqrt(own * rows * cols)

    f32, bf16, i32 = jnp.float32, jnp.bfloat16, jnp.int32
    vmem = pl.BlockSpec(memory_space=pltpu.VMEM)
    r1, c1 = (rows - 1,), (cols - 1,)
    dma = pltpu.SemaphoreType.DMA
    out_shape = (
        jax.ShapeDtypeStruct((own, width), f32),
        jax.ShapeDtypeStruct((own, width), f32),
        jax.ShapeDtypeStruct((width, width), f32),
        jax.ShapeDtypeStruct((1, width), f32),
    )
    outs = pl.pallas_call(
        functools.partial(kernel, rows, cols, norm),
        out_shape=tuple(pltpu.VMEM(out.shape, out.dtype) for out in out_shape),
        in_specs=[pl.BlockSpec(memory_space=pltpu.HBM)] * 8,
        out_specs=(vmem, vmem, vmem, vmem),
        scratch_shapes=[
            pltpu.VMEM((own, width), f32),
            pltpu.VMEM((width, width), f32),
            pltpu.VMEM((1, width), f32),
            pltpu.VMEM((1, own), f32),
            pltpu.VMEM((own, width), f32),
            pltpu.VMEM((1, slots), i32),
            pltpu.VMEM((1,), i32),
            pltpu.VMEM((places, 128), i32),
            pltpu.SMEM((places, 128), i32),
            pltpu.VMEM((slots + 1, tile, tile), bf16),
            pltpu.VMEM((rows * sub, tile, cols * own), bf16),
            pltpu.VMEM((cols * own, rows * own), bf16),
            pltpu.VMEM((cols, own, width), bf16),
            pltpu.VMEM((rows - 1, own, width), WIRE),
            pltpu.VMEM((rows - 1, own, width), WIRE),
            pltpu.VMEM((rows, own, width), bf16),
            pltpu.VMEM((3 * width, width), bf16),
            pltpu.VMEM((3 * width, width), bf16),
            pltpu.VMEM((cols, own, width), f32),
            pltpu.VMEM((cols - 1, own, width), WIRE),
            pltpu.VMEM((cols - 1, own, width), WIRE),
            pltpu.VMEM((cols, piece + 8, width), f32),
            pltpu.VMEM((rows, piece + 16, width), WIRE),
            pltpu.VMEM((cols, piece + 8, width), f32),
            pltpu.VMEM((cols, piece, width), f32),
            dma((7,)), dma, dma, dma(c1), dma(c1), dma(r1), dma(r1), dma(r1), dma(r1),
            dma(c1), dma(c1), dma(c1), dma(c1), dma(r1), dma(r1), dma(c1), dma(c1),
        ],
        compiler_params=pltpu.CompilerParams(collective_id=0, has_side_effects=True),
        name="graph_layer",
    )(
        features, weight, layer_bias.reshape(1, width), degree_scale.reshape(1, own),
        cotangent, tile_values.reshape(slots, tile, tile), tile_slots.reshape(1, slots),
        tile_count.reshape(1),
    )
    outs = pl.pallas_call(
        write_out,
        out_shape=out_shape,
        in_specs=[vmem] * 4,
        out_specs=[pl.BlockSpec(memory_space=pltpu.HBM)] * 4,
        scratch_shapes=[dma((4,))],
        name="write_out",
    )(*[pltpu.with_memory_space_constraint(out, pltpu.VMEM) for out in outs])
    return (outs[0], outs[1], outs[2], outs[3].reshape(width))


def solution(mesh):
    return jax.shard_map(
        local,
        mesh=mesh,
        in_specs=(
            P(("row", "col"), None),
            P(),
            P(),
            P(("row", "col")),
            P("row", "col", None, None, None),
            P("row", "col", None),
            P("row", "col"),
            P(("row", "col"), None),
        ),
        out_specs=(P(("row", "col"), None), P(("row", "col"), None), P(), P()),
        check_vma=False,
    )
```
